32 devices in a mesh: dp: 2 (over y), ctx: 4 (over x, core), tensor: 4 (over z).
Axes of the slice: x: 2, y: 2, z: 4, core: 2. Of those that a mesh axis runs over, the one named last changes fastest.
Arguments:
- hidden: bfloat16 [4, 1024, 2048], P('dp', 'ctx'), may hold values from -6 to 6
- cotangent: bfloat16 [4, 1024, 2048], P('dp', 'ctx'), may hold values from -6 to 6
- segment_ids: int32 [4, 1024], P('dp', 'ctx'), may hold values from 0 to 5, never falling along the last dimension, each value on 1 to 800 neighbouring positions
- attn_gain: bfloat16 [2048], P(('dp', 'ctx')), may hold values from 0.5 to 1.5
- w_query: bfloat16 [2048, 2048], P(('dp', 'ctx'), 'tensor'), may hold values from -0.125 to 0.125
- key_matrix: bfloat16 [2048, 256], P(('dp', 'ctx'), 'tensor'), may hold values from -0.125 to 0.125
- value_matrix: bfloat16 [2048, 256], P(('dp', 'ctx'), 'tensor'), may hold values from -0.125 to 0.125
- w_out: bfloat16 [2048, 2048], P('tensor', ('dp', 'ctx')), may hold values from -1 to 1
- mlp_gain: bfloat16 [2048], P(('dp', 'ctx')), may hold values from 0.5 to 1.5
- w_gate: bfloat16 [2048, 5632], P(('dp', 'ctx'), 'tensor'), may hold values from -0.125 to 0.125
- w_up: bfloat16 [2048, 5632], P(('dp', 'ctx'), 'tensor'), may hold values from -0.125 to 0.125
- w_down: bfloat16 [5632, 2048], P('tensor', ('dp', 'ctx')), may hold values from -0.078125 to 0.078125
Outputs:
- layer_out: bfloat16 [4, 1024, 2048], P('dp', 'ctx')
- d_hidden: float32 [4, 1024, 2048], P('dp', 'ctx')
- grad_attn_gain: float32 [2048], P(('dp', 'ctx'))
- grad_query: float32 [2048, 2048], P(('dp', 'ctx'), 'tensor')
- grad_key: float32 [2048, 256], P(('dp', 'ctx'), 'tensor')
- grad_value: float32 [2048, 256], P(('dp', 'ctx'), 'tensor')
- grad_out: float32 [2048, 2048], P('tensor', ('dp', 'ctx'))
- grad_mlp_gain: float32 [2048], P(('dp', 'ctx'))
- grad_gate: float32 [2048, 5632], P(('dp', 'ctx'), 'tensor')
- grad_up: float32 [2048, 5632], P(('dp', 'ctx'), 'tensor')
- grad_down: float32 [5632, 2048], P('tensor', ('dp', 'ctx'))
The draws below stay inside these ranges and needn't reach their ends.
Inputs may be any that keep to these rules, and one draw needn't show every extreme that they name: `segment_ids`: along each sequence the ids never fall, every id appears, each document holds 1 to 800 tokens, and one holds exactly 800.
All inputs are finite; a program needn't handle non-finite values.
Results may differ from the reference program's by a relative error of at most 0.013.
Values may be sent and summed in bfloat16 or wider, within the bound.
No kernel may reach another device: no remote copies, remote signals or barrier semaphores. Data moves between devices by JAX's collectives and lax.ppermute only.
A program may use at most 192 MiB of HBM per device.

```python
import math
import jax
import jax.numpy as jnp
import numpy as np
from jax import lax

MODEL_DIMENSION = 2048
QUERY_HEADS = 32
SHARED_KV_HEADS = 4
HEAD_DIMENSION = 64
FF = 5632
MB = 2
SEQ_MB = 1
DOCS = 6
SEQUENCE_TOKENS = 1024
SEQS = 4
DOC_MOST = 800
N_DP = 2


def spiked(entries, rng, source, target, parts, factor):
    owner, partner = [(jnp.arange(entries.shape[position]) // (entries.shape[position] // parts)).reshape([-1 if axis == position else 1 for axis in range(entries.ndim)]) for position in (source, target)]
    chosen = jax.random.permutation(rng, parts)[partner]
    strong = (owner == chosen) | (owner == (partner + parts // 2) % parts)
    return jnp.where(strong, factor * entries, entries)


def level_of(stream_key, extent, pieces, smallest, top_value):
    loudness = 1.0
    for dim, parts in pieces:
        steps = jax.random.uniform(jax.random.fold_in(jax.random.fold_in(stream_key, 6), dim), (parts,), jnp.float32, smallest / len(pieces), top_value / len(pieces))
        loudness = loudness * jnp.repeat(jnp.exp(steps), extent[dim] // parts).reshape((-1,) + (1,) * (len(extent) - 1 - dim))
    return loudness


def profile(number_of, total, bound, lean):
    loads = [(1 << 20) // math.isqrt(rank ** lean) + 1 for rank in range(2, number_of + 1)]
    surplus, counts = total - bound - (number_of - 1), [1] * (number_of - 1)
    while surplus > 0:
        free = [i for i in range(number_of - 1) if counts[i] < bound]
        whole, left = sum([loads[i] for i in free]), surplus
        for i in free:
            addition = min(bound - counts[i], max(1, left * loads[i] // whole), surplus)
            counts[i] = counts[i] + addition
            surplus = surplus - addition
    return np.array([bound] + counts)


def ragged(key, amount, total, reach, skew):
    if amount == 2:
        one = jax.random.randint(key, (), max(1, total - reach), min(reach, total - 1) + 1)
        return jnp.stack([one, total - one])
    sizes = jnp.asarray(profile(amount, total, reach, skew), jnp.int32)
    couples = (amount - 1) // 2
    giver, sink = sizes[1:1 + 2 * couples:2], sizes[2:2 + 2 * couples:2]
    slack = jnp.minimum(giver - 1, reach - sink)
    moved = jax.random.randint(jax.random.fold_in(key, 1), (couples,), 0, 1 << 20) % (slack + 1)
    sizes = sizes.at[1:1 + 2 * couples:2].set(giver - moved).at[2:2 + 2 * couples:2].set(sink + moved)
    return sizes[jax.random.permutation(jax.random.fold_in(key, 2), amount)]


def bell_draw(stream_key, dims, scale, bound, pieces=(), held_as=jnp.bfloat16):
    values = scale * jax.random.normal(stream_key, dims, jnp.float32)
    if pieces:
        values = values * level_of(stream_key, dims, pieces, -0.22, 0.18)
    return jnp.clip(values, -bound, bound).astype(held_as)


def noise_with(stream_key, shape, spread, limit, shards, heavy, kind=jnp.bfloat16):
    values = spread * jax.random.normal(stream_key, shape, jnp.float32)
    if shards:
        values = values * level_of(stream_key, shape, shards, -0.22, 0.18)
    return jnp.clip(spiked(values, jax.random.fold_in(stream_key, 3), *heavy), -limit, limit).astype(kind)


def setup_inputs(seed: int = 0) -> dict:
    streams_of = jax.random.split(jax.random.key(seed), 13)
    hidden = bell_draw(streams_of[0], (SEQS, SEQUENCE_TOKENS, MODEL_DIMENSION), 1.0, 6.0, ((0, 2), (1, 4)))
    cotangent = noise_with(streams_of[1], (SEQS, SEQUENCE_TOKENS, MODEL_DIMENSION), 1.0, 6.0, ((0, 2), (1, 4)), (0, 2, 2, 2.0))
    segment_ids = jax.vmap(lambda own: jnp.searchsorted(jnp.cumsum(ragged(own, DOCS, SEQUENCE_TOKENS, DOC_MOST, 2)), jnp.arange(SEQUENCE_TOKENS), side="right"))(jax.random.split(streams_of[2], SEQS)).reshape((SEQS, SEQUENCE_TOKENS)).astype(jnp.int32)
    attn_gain = jnp.clip(1.0 + 0.1 * jax.random.normal(streams_of[3], (MODEL_DIMENSION,), jnp.float32), 0.5, 1.5).astype(jnp.bfloat16)
    w_query = bell_draw(streams_of[4], (MODEL_DIMENSION, QUERY_HEADS * HEAD_DIMENSION), MODEL_DIMENSION ** -0.5, 0.125, ((0, 8), (1, 4)))
    key_matrix = bell_draw(streams_of[5], (MODEL_DIMENSION, SHARED_KV_HEADS * HEAD_DIMENSION), MODEL_DIMENSION ** -0.5, 0.125, ((0, 8), (1, 4)))
    value_matrix = bell_draw(streams_of[6], (MODEL_DIMENSION, SHARED_KV_HEADS * HEAD_DIMENSION), MODEL_DIMENSION ** -0.5, 0.125, ((0, 8), (1, 4)))
    w_out = bell_draw(streams_of[7], (QUERY_HEADS * HEAD_DIMENSION, MODEL_DIMENSION), (max(QUERY_HEADS * HEAD_DIMENSION // 64, 1)) ** -0.5, 1.0, ((0, 4), (1, 8)))
    mlp_gain = jnp.clip(1.0 + 0.1 * jax.random.normal(streams_of[8], (MODEL_DIMENSION,), jnp.float32), 0.5, 1.5).astype(jnp.bfloat16)
    w_gate = bell_draw(streams_of[9], (MODEL_DIMENSION, FF), MODEL_DIMENSION ** -0.5, 0.125, ((0, 8), (1, 4)))
    w_up = bell_draw(streams_of[10], (MODEL_DIMENSION, FF), MODEL_DIMENSION ** -0.5, 0.125, ((0, 8), (1, 4)))
    w_down = bell_draw(streams_of[11], (FF, MODEL_DIMENSION), FF ** -0.5, 0.078125, ((0, 4), (1, 8)))
    return dict(hidden=hidden, cotangent=cotangent, segment_ids=segment_ids, attn_gain=attn_gain, w_query=w_query, key_matrix=key_matrix, value_matrix=value_matrix, w_out=w_out, mlp_gain=mlp_gain, w_gate=w_gate, w_up=w_up, w_down=w_down)


@jax.custom_vjp
def low(v):
    return lax.optimization_barrier(v.astype(jnp.bfloat16)).astype(jnp.float32)

@jax.custom_vjp
def reduced_backward(v):
    return v

def low_keep(v):
    return (low(v), None)

def low_pass(kept, grad):
    return (grad,)

def back_keep(v):
    return (v, None)

def back_low(kept, grad):
    return (low(grad),)
low.defvjp(low_keep, low_pass)
reduced_backward.defvjp(back_keep, back_low)
EPSILON = 1e-05
THETA = 10000.0
NEG_FILL = -1e+30

def matrix_multiply(left_side, right_side):
    return jnp.dot(left_side, right_side, precision=lax.Precision.HIGHEST)

def inv_rms(values):
    return lax.rsqrt(lax.optimization_barrier(jnp.mean(values * values, axis=-1, keepdims=True)) + EPSILON)

def angles_for(positions, head_size):
    freq_index = jnp.arange(head_size // 2, dtype=jnp.float32)
    inverse = jnp.power(jnp.float32(THETA), -2.0 * freq_index / head_size)
    angle_table = positions.astype(jnp.float32)[:, None] * inverse[None, :]
    return (jnp.cos(angle_table), jnp.sin(angle_table))

def rotary(vectors, cosine, sine_table):
    half_size = vectors.shape[-1] // 2
    front_half = vectors[..., :half_size]
    back_half = vectors[..., half_size:]
    return jnp.concatenate([front_half * cosine - back_half * sine_table, back_half * cosine + front_half * sine_table], axis=-1)

def layer(source, attn_gain, w_query, key_matrix, value_matrix, w_out, mlp_gain, w_gate, w_up, w_down, allowed):
    sequence_count = source.shape[0]
    heads_per_group = QUERY_HEADS // SHARED_KV_HEADS
    first_normalized = low(source * inv_rms(source) * attn_gain)
    query_proj = reduced_backward(matrix_multiply(first_normalized, w_query)).reshape(sequence_count, SEQUENCE_TOKENS, QUERY_HEADS, HEAD_DIMENSION)
    projected_keys = reduced_backward(matrix_multiply(first_normalized, key_matrix)).reshape(sequence_count, SEQUENCE_TOKENS, SHARED_KV_HEADS, HEAD_DIMENSION)
    projected_values = reduced_backward(matrix_multiply(first_normalized, value_matrix)).reshape(sequence_count, SEQUENCE_TOKENS, SHARED_KV_HEADS, HEAD_DIMENSION)
    cosine, sine_table = angles_for(jnp.arange(SEQUENCE_TOKENS), HEAD_DIMENSION)
    query_rows = low(rotary(query_proj, cosine[:, None], sine_table[:, None]))
    keys_rot = low(rotary(projected_keys, cosine[:, None], sine_table[:, None]))
    values_low = low(projected_values)
    query_head_rows = jnp.transpose(query_rows.reshape(sequence_count, SEQUENCE_TOKENS, SHARED_KV_HEADS, heads_per_group, HEAD_DIMENSION), (2, 0, 3, 1, 4))
    key_heads = jnp.transpose(keys_rot, (2, 0, 1, 3))
    value_heads = jnp.transpose(values_low, (2, 0, 1, 3))

    def head_group(block_items):
        query_block, key_block, value_block = block_items
        logits = reduced_backward(jnp.einsum('gaqd,gkd->gaqk', query_block, key_block, precision=lax.Precision.HIGHEST) * HEAD_DIMENSION ** (-0.5))
        logits = jnp.where(allowed[:, None], logits, NEG_FILL)
        weights_low = low(jax.nn.softmax(logits, axis=-1))
        return jnp.einsum('gaqk,gkd->gaqd', weights_low, value_block, precision=lax.Precision.HIGHEST)
    mixed = lax.map(jax.checkpoint(head_group), (query_head_rows, key_heads, value_heads))
    heads_out = low(reduced_backward(jnp.transpose(mixed, (1, 3, 0, 2, 4)).reshape(sequence_count, SEQUENCE_TOKENS, QUERY_HEADS * HEAD_DIMENSION)))
    attn_out = reduced_backward(matrix_multiply(heads_out, w_out))
    residual = source + attn_out
    normed_two = low(residual * inv_rms(residual) * mlp_gain)
    gate_pre = reduced_backward(matrix_multiply(normed_two, w_gate))
    up_pre = reduced_backward(matrix_multiply(normed_two, w_up))
    activated = low(jax.nn.silu(gate_pre) * up_pre)
    return residual + reduced_backward(matrix_multiply(activated, w_down))

def reference(hidden, cotangent, segment_ids, attn_gain, w_query, key_matrix, value_matrix, w_out, mlp_gain, w_gate, w_up, w_down):
    params = tuple((member.astype(jnp.float32) for member in (attn_gain, w_query, key_matrix, value_matrix, w_out, mlp_gain, w_gate, w_up, w_down)))
    group_seqs = MB * SEQ_MB
    inputs = hidden.astype(jnp.float32).reshape(N_DP, group_seqs, SEQUENCE_TOKENS, MODEL_DIMENSION)
    grads_in = cotangent.astype(jnp.float32).reshape(N_DP, group_seqs, SEQUENCE_TOKENS, MODEL_DIMENSION)
    segments = segment_ids.astype(jnp.int32).reshape(N_DP, group_seqs, SEQUENCE_TOKENS)
    positions = jnp.arange(SEQUENCE_TOKENS)

    def step_group(running, block_items):
        source, grad_top, seg_block = block_items
        allowed = (seg_block[:, :, None] == seg_block[:, None, :]) & (positions[:, None] >= positions[None, :])

        def apply_layer(source_in, *weights):
            return layer(source_in, *weights, allowed)
        result, pull_back = jax.vjp(apply_layer, source, *params)
        pulled = pull_back(grad_top)
        running = tuple((earlier + addend for earlier, addend in zip(running, pulled[1:])))
        return (running, (result, pulled[0]))
    initial = tuple((jnp.zeros_like(member) for member in params))
    summed, (results, input_grads) = lax.scan(step_group, initial, (inputs, grads_in, segments))
    return (results.reshape(SEQS, SEQUENCE_TOKENS, MODEL_DIMENSION).astype(jnp.bfloat16), input_grads.reshape(SEQS, SEQUENCE_TOKENS, MODEL_DIMENSION), summed[0], summed[1], summed[2], summed[3], summed[4], summed[5], summed[6], summed[7], summed[8])
```

```python
import jax
import jax.numpy as jnp
from jax import lax
from jax.sharding import PartitionSpec as P

MB = 2


EPSILON = 1e-05
THETA = 10000.0
NEG_FILL = -1e30
AXES = ("dp", "ctx", "tensor")
BF = jnp.bfloat16
F32 = jnp.float32


def dot(a, b):
    return lax.dot_general(a, b, (((1,), (0,)), ((), ())), preferred_element_type=F32)


def dot_t(a, b):
    return lax.dot_general(a, b, (((1,), (1,)), ((), ())), preferred_element_type=F32)


def dot_rows(a, b):
    return lax.dot_general(a, b, (((0,), (0,)), ((), ())), preferred_element_type=F32)


def inv_rms(values):
    return lax.rsqrt(jnp.mean(values * values, axis=-1, keepdims=True) + EPSILON)


def angles_for(positions, head_size):
    freq_index = jnp.arange(head_size // 2, dtype=jnp.float32)
    inverse = jnp.power(jnp.float32(THETA), -2.0 * freq_index / head_size)
    angle_table = positions.astype(jnp.float32)[:, None] * inverse[None, :]
    return (jnp.cos(angle_table), jnp.sin(angle_table))


def rotary(vectors, cosine, sine_table):
    half_size = vectors.shape[-1] // 2
    front_half = vectors[..., :half_size]
    back_half = vectors[..., half_size:]
    return jnp.concatenate(
        [
            front_half * cosine - back_half * sine_table,
            back_half * cosine + front_half * sine_table,
        ],
        axis=-1,
    )


def make_fast():
    def index(y, x, core, z):
        return (y * 4 + x * 2 + core) * 4 + z

    def pairs(target):
        return [
            (index(y, x, core, z), index(*target(y, x, core, z)))
            for y in range(2)
            for x in range(2)
            for core in range(2)
            for z in range(4)
        ]

    across_core = pairs(lambda y, x, c, z: (y, x, 1 - c, z))
    across_x = pairs(lambda y, x, c, z: (y, 1 - x, c, z))
    first_way = pairs(lambda y, x, c, z: (y, 1 - x, c, z) if c == 0 else (1 - y, x, c, z))
    second_way = pairs(lambda y, x, c, z: (1 - y, x, c, z) if c == 0 else (y, 1 - x, c, z))
    z_pair = pairs(lambda y, x, c, z: (y, x, c, z ^ 1))
    z_mirror = pairs(lambda y, x, c, z: (y, x, c, 3 - z))

    def send(value, table):
        return lax.ppermute(value, AXES, table)

    masks = ((0, 4, 2, 6, 1, 3, 5, 7), (0, 2, 4, 6, 1, 5, 3, 7))

    def after(value, *earlier):
        return lax.optimization_barrier((value,) + earlier)[0]

    def gather_start(shard):
        other = send(shard, across_core)
        near = send(jnp.stack([shard, other]), first_way)
        return (shard, other, near)

    def gather_finish(state):
        shard, other, near = state
        side = send(near, across_core)
        diagonal = send(side[1], first_way)
        diagonal_other = send(diagonal, across_core)
        return (shard, side[1], near[0], diagonal, other, near[1], side[0], diagonal_other)

    def scatter_sum(same, opposite):
        arrived = send(opposite, across_core)
        chip = same.astype(F32) + arrived.astype(F32)
        arrived = send(chip[2:].astype(BF), first_way)
        line = chip[:2] + arrived.astype(F32)
        arrived = send(line[1].astype(BF), second_way)
        return line[0] + arrived.astype(F32)

    def scatter_sum_small(blocks):
        arrived = send(blocks[4:], across_core)
        chip = blocks[:4] + arrived
        arrived = send(chip[2:], first_way)
        line = chip[:2] + arrived
        arrived = send(line[1], second_way)
        return line[0] + arrived

    def reduce_z(partial):
        half = partial.shape[0] // 2
        arrived = send(partial[half:], z_pair)
        two = (partial[:half].astype(F32) + arrived.astype(F32)).astype(BF)
        arrived = send(two, z_mirror)
        return two.astype(F32) + arrived.astype(F32)

    def share_z(owned):
        return jnp.concatenate([owned, send(owned, z_pair)], axis=0)

    def per_device(
        hidden,
        cotangent,
        segment_ids,
        attn_gain,
        w_query,
        key_matrix,
        value_matrix,
        w_out,
        mlp_gain,
        w_gate,
        w_up,
        w_down,
    ):
        span = hidden.shape[1]
        width = hidden.shape[2]
        rows = w_query.shape[0]
        head_size = key_matrix.shape[1]
        local_heads = w_query.shape[1] // head_size
        q_cols = w_query.shape[1]
        qkv_cols = q_cols + 2 * head_size
        ff = w_gate.shape[1]
        half = span // 2
        score_scale = head_size ** (-0.5)
        context = lax.axis_index("ctx")
        core = lax.rem(context, 2)
        block = lax.axis_index("dp") * 4 + context
        depth = lax.axis_index("tensor")
        flip = jnp.where((depth == 0) | (depth == 3), 0, 1)
        mask_table = jnp.array(masks, jnp.int32)
        my_masks = mask_table[core]
        owner_of = [lax.bitwise_xor(block, my_masks[p]) for p in range(8)]
        inverse = jnp.array([[m.index(v) for v in range(8)] for m in masks], jnp.int32)[core]
        place_of = [inverse[lax.bitwise_xor(block, b)] for b in range(8)]

        def to_local(array):
            top = lax.dynamic_slice_in_dim(array, flip * half, half, 1)
            low = lax.dynamic_slice_in_dim(array, (1 - flip) * half, half, 1)
            array = jnp.concatenate([top, low], axis=1)
            return jnp.concatenate(
                [lax.dynamic_slice_in_dim(array, o * rows, rows, 2) for o in owner_of], axis=2
            )

        def from_local(array):
            top = lax.dynamic_slice_in_dim(array, flip * half, half, 0)
            low = lax.dynamic_slice_in_dim(array, (1 - flip) * half, half, 0)
            array = jnp.concatenate([top, low], axis=0)
            return jnp.concatenate(
                [lax.dynamic_slice_in_dim(array, o * rows, rows, 1) for o in place_of], axis=1
            )

        seg_rows = jnp.concatenate(
            [
                lax.dynamic_slice_in_dim(segment_ids, flip * half, half, 1),
                lax.dynamic_slice_in_dim(segment_ids, (1 - flip) * half, half, 1),
            ],
            axis=1,
        ).astype(BF)
        extra = jnp.zeros((16, qkv_cols), BF)
        extra = extra.at[0, :rows].set(attn_gain)
        extra = extra.at[1, :rows].set(mlp_gain)
        extra = extra.at[2, : MB * span].set(seg_rows.reshape(-1))
        shard_one = jnp.concatenate(
            [jnp.concatenate([w_query, key_matrix, value_matrix], axis=1), extra], axis=0
        )
        one = gather_finish(gather_start(shard_one))
        shard_two = after(w_out.T, one[2])
        two = gather_finish(gather_start(shard_two))
        shard_three = after(jnp.concatenate([w_gate, w_up], axis=1), one[3])
        three = gather_finish(gather_start(shard_three))
        shard_four = after(w_down.T, three[2])
        four = gather_finish(gather_start(shard_four))

        qkv_w = jnp.concatenate([piece[:rows] for piece in one], axis=0)
        gain_one = jnp.concatenate([piece[rows, :rows] for piece in one]).astype(F32)
        gain_two = jnp.concatenate([piece[rows + 1, :rows] for piece in one]).astype(F32)
        seg_of = [piece[rows + 2, : MB * span].reshape(MB, span) for piece in one]
        seg_keys = [
            seg_of[0],
            seg_of[4],
            jnp.where(core == 0, seg_of[2], seg_of[1]),
            jnp.where(core == 0, seg_of[5], seg_of[6]),
        ]
        seg_keys = jnp.concatenate(seg_keys, axis=1)
        out_w = jnp.concatenate(two, axis=0)
        gate_up_w = jnp.concatenate(three, axis=0)
        down_w = jnp.concatenate(four, axis=0)

        token = jnp.arange(span, dtype=jnp.int32)
        token = jnp.where(token < half, token + flip * half, token - flip * half)
        positions_q = context * span + token
        positions_k = jnp.concatenate(
            [lax.bitwise_xor(context, j) * span + token for j in range(4)]
        )
        cosine, sine = angles_for(positions_q, head_size)
        cos_heads = cosine[:, None, :]
        sin_heads = sine[:, None, :]
        causal = positions_q[:, None] >= positions_k[None, :]

        hidden_local = to_local(hidden)
        cot_local = to_local(cotangent)

        def key_value_gather(pair):
            both = jnp.stack([pair, send(pair, across_core)])
            far = send(both, across_x)
            return jnp.concatenate([both[0], both[1], far[0], far[1]], axis=0)

        def key_value_scatter(terms):
            blocks = terms.reshape(2, 2, span, terms.shape[1])
            arrived = send(blocks[:, 1].astype(BF), across_core)
            chip = blocks[:, 0] + arrived.astype(F32)
            arrived = send(chip[1].astype(BF), across_x)
            return chip[0] + arrived.astype(F32)

        def attention(m):
            source = hidden_local[m].astype(F32)
            inv_one = inv_rms(source)
            normed = (source * inv_one * gain_one).astype(BF)
            proj = dot(normed, qkv_w)
            queries = rotary(
                proj[:, :q_cols].reshape(span, local_heads, head_size), cos_heads, sin_heads
            ).astype(BF)
            keys_own = rotary(proj[:, q_cols : q_cols + head_size], cosine, sine)
            pair = jnp.concatenate([keys_own, proj[:, q_cols + head_size :]], axis=1).astype(BF)
            pairs_all = key_value_gather(pair)
            keys, values = pairs_all[:, :head_size], pairs_all[:, head_size:]
            allowed = (seg_rows[m][:, None] == seg_keys[m][None, :]) & causal
            logits = jnp.einsum("qhd,kd->hqk", queries, keys, preferred_element_type=F32)
            logits = jnp.where(allowed[None], logits * score_scale, NEG_FILL)
            peak = jnp.max(logits, axis=-1, keepdims=True)
            shifted = jnp.exp(logits - peak)
            totals = jnp.sum(shifted, axis=-1, keepdims=True)
            probs = (shifted / totals).astype(BF)
            log_norm = peak + jnp.log(totals)
            heads = jnp.einsum("hqk,kd->qhd", probs, values, preferred_element_type=F32)
            heads = heads.reshape(span, q_cols).astype(BF)
            partial = dot_t(heads, out_w).astype(BF)
            attn_own = reduce_z(partial)
            source_own = source[:half]
            residual = source_own + attn_own
            inv_two = inv_rms(residual)
            normed_two = share_z((residual * inv_two * gain_two).astype(BF))
            return dict(
                normed=normed,
                inv_one=inv_one[:half],
                source=source_own,
                queries=queries,
                keys=keys,
                values=values,
                allowed=allowed,
                log_norm=log_norm,
                heads=heads,
                residual=residual,
                inv_two=inv_two,
                normed_two=normed_two,
            )

        def norm_back(grad_normed, source, inv_scale, gain_full):
            normalized = source * inv_scale
            scaled = grad_normed * gain_full
            middle = jnp.mean(scaled * normalized, axis=-1, keepdims=True)
            gain_term = jnp.sum(grad_normed * normalized, axis=0)
            return (inv_scale * (scaled - normalized * middle), gain_term)

        def mlp(m, st):
            normed_two = st["normed_two"]
            both = dot(normed_two, gate_up_w)
            gate_pre, up_pre = both[:, :ff], both[:, ff:]
            sig = jax.nn.sigmoid(gate_pre)
            silu_gate = gate_pre * sig
            activated = (silu_gate * up_pre).astype(BF)
            cot = cot_local[m]
            d_act = dot(cot, down_w)
            d_gate = (d_act * up_pre * sig * (1.0 + gate_pre * (1.0 - sig))).astype(BF)
            d_up = (d_act * silu_gate).astype(BF)
            d_both = jnp.concatenate([d_gate, d_up], axis=1)
            partial = dot_t(d_both, gate_up_w).astype(BF)
            d_normed_two = reduce_z(partial)
            d_norm, gain_term = norm_back(d_normed_two, st["residual"], st["inv_two"], gain_two)
            d_residual = cot[:half].astype(F32) + d_norm
            d_low = share_z(d_residual.astype(BF))
            mlp_own = reduce_z(dot_t(activated, down_w).astype(BF))
            out = share_z((st["residual"] + mlp_own).astype(BF))
            return dict(
                activated=activated,
                d_both=d_both,
                gain_term=gain_term,
                d_residual=d_residual,
                d_low=d_low,
                out=from_local(out),
            )

        def attention_back(m, st, ml):
            d_heads = dot(ml["d_low"], out_w).astype(BF).reshape(span, local_heads, head_size)
            queries, keys, values = st["queries"], st["keys"], st["values"]
            again = jnp.einsum("qhd,kd->hqk", queries, keys, preferred_element_type=F32)
            again = jnp.where(st["allowed"][None], again * score_scale, NEG_FILL)
            probs = jnp.exp(again - st["log_norm"])
            probs_low = probs.astype(BF)
            d_probs = jnp.einsum("qhd,kd->hqk", d_heads, values, preferred_element_type=F32)
            row_delta = jnp.sum(probs * d_probs, axis=-1, keepdims=True)
            d_scores = (probs * (d_probs - row_delta)).astype(BF)
            d_query = (
                jnp.einsum("hqk,kd->qhd", d_scores, keys, preferred_element_type=F32) * score_scale
            )
            key_terms = (
                jnp.einsum("hqk,qhd->kd", d_scores, queries, preferred_element_type=F32)
                * score_scale
            )
            value_terms = jnp.einsum("hqk,qhd->kd", probs_low, d_heads, preferred_element_type=F32)
            kv = key_value_scatter(jnp.concatenate([key_terms, value_terms], axis=1))
            d_query_proj = rotary(d_query, cos_heads, -sin_heads).reshape(span, q_cols)
            d_key_proj = rotary(kv[:, :head_size], cosine, -sine)
            d_proj = jnp.concatenate([d_query_proj, d_key_proj, kv[:, head_size:]], axis=1)
            d_proj = d_proj.astype(BF)
            d_normed = reduce_z(dot_t(d_proj, qkv_w).astype(BF))
            d_norm, gain_term = norm_back(d_normed, st["source"], st["inv_one"], gain_one)
            d_hidden = share_z((ml["d_residual"] + d_norm).astype(BF))
            return dict(d_proj=d_proj, gain_term=gain_term, d_hidden=from_local(d_hidden))

        st = [attention(m) for m in range(MB)]
        ml = [mlp(m, st[m]) for m in range(MB)]
        ab = [attention_back(m, st[m], ml[m]) for m in range(MB)]

        def joined(parts):
            return jnp.concatenate(parts, axis=0)

        def weight_grad(left, right):
            count = left.shape[1] // 2
            same = dot_rows(left[:, :count], right).astype(BF).reshape(4, rows, -1)
            opposite = dot_rows(left[:, count:], right).astype(BF).reshape(4, rows, -1)
            return scatter_sum(same, opposite)

        grad_down = weight_grad(
            cot_local.reshape(MB * span, width), joined([s["activated"] for s in ml])
        )
        grad_gate_up = weight_grad(
            joined([s["normed_two"] for s in st]), joined([s["d_both"] for s in ml])
        )
        grad_out = weight_grad(
            joined([s["d_low"] for s in ml]), joined([s["heads"] for s in st])
        )
        grad_qkv = weight_grad(
            joined([s["normed"] for s in st]), joined([s["d_proj"] for s in ab])
        )
        gains = jnp.stack(
            [ab[0]["gain_term"] + ab[1]["gain_term"], ml[0]["gain_term"] + ml[1]["gain_term"]]
        )
        gains = jnp.transpose(gains.reshape(2, 8, rows), (1, 0, 2))
        gains = scatter_sum_small(gains)
        gains = gains + send(gains, z_pair)

        return (
            jnp.stack([s["out"] for s in ml]),
            jnp.stack([s["d_hidden"] for s in ab]).astype(F32),
            gains[0],
            grad_qkv[:, :q_cols],
            grad_qkv[:, q_cols : q_cols + head_size],
            grad_qkv[:, q_cols + head_size :],
            grad_out.T,
            gains[1],
            grad_gate_up[:, :ff],
            grad_gate_up[:, ff:],
            grad_down.T,
        )

    return per_device


def norm_back(grad_normed, source, inv_scale, gain_full):
    normalized = source * inv_scale
    scaled = grad_normed * gain_full
    middle = jnp.mean(scaled * normalized, axis=-1, keepdims=True)
    gain_term = jnp.sum(grad_normed * normalized, axis=(0, 1))
    return (inv_scale * (scaled - normalized * middle), gain_term)


def collect(shards):
    return (
        lax.all_gather(shards[0], ("dp", "ctx"), axis=0, tiled=True),
        lax.all_gather(shards[1], ("dp", "ctx"), axis=0, tiled=True),
        lax.all_gather(shards[2], ("dp", "ctx"), axis=0, tiled=True),
        lax.all_gather(shards[3], ("dp", "ctx"), axis=0, tiled=True),
        lax.all_gather(shards[4], ("dp", "ctx"), axis=1, tiled=True),
        lax.all_gather(shards[5], ("dp", "ctx"), axis=0, tiled=True),
        lax.all_gather(shards[6], ("dp", "ctx"), axis=0, tiled=True),
        lax.all_gather(shards[7], ("dp", "ctx"), axis=0, tiled=True),
        lax.all_gather(shards[8], ("dp", "ctx"), axis=1, tiled=True),
    )


def contract(left_side, right_side):
    return jnp.einsum("stc,stf->cf", left_side, right_side, preferred_element_type=jnp.float32)


def project_back(grad_rows, weight_full):
    return jnp.einsum("stf,cf->stc", grad_rows, weight_full, preferred_element_type=jnp.float32)


def per_device_general(
    hidden,
    cotangent,
    segment_ids,
    attn_gain,
    w_query,
    key_matrix,
    value_matrix,
    w_out,
    mlp_gain,
    w_gate,
    w_up,
    w_down,
):
    shards = (attn_gain, w_query, key_matrix, value_matrix, w_out, mlp_gain, w_gate, w_up, w_down)
    span_len = hidden.shape[1]
    model_width = hidden.shape[2]
    seq_count = hidden.shape[0] // MB
    head_size = key_matrix.shape[1]
    local_heads = w_query.shape[1] // head_size
    seq_len = span_len * lax.axis_size("ctx")
    score_scale = head_size ** (-0.5)
    positions_q = lax.axis_index("ctx") * span_len + jnp.arange(span_len, dtype=jnp.int32)
    positions_k = jnp.arange(seq_len, dtype=jnp.int32)
    cosine, sine_table = angles_for(positions_q, head_size)
    cos_heads = cosine[:, None, :]
    sin_heads = sine_table[:, None, :]
    causal = positions_q[:, None] >= positions_k[None, :]
    grad_list = [
        jnp.zeros((model_width,), jnp.float32),
        jnp.zeros((model_width, w_query.shape[1]), jnp.float32),
        jnp.zeros((model_width, key_matrix.shape[1]), jnp.float32),
        jnp.zeros((model_width, value_matrix.shape[1]), jnp.float32),
        jnp.zeros((w_out.shape[0], model_width), jnp.float32),
        jnp.zeros((model_width,), jnp.float32),
        jnp.zeros((model_width, w_gate.shape[1]), jnp.float32),
        jnp.zeros((model_width, w_up.shape[1]), jnp.float32),
        jnp.zeros((w_down.shape[0], model_width), jnp.float32),
    ]
    outputs = []
    input_grads = []
    for batch_index in range(MB):
        gathered = collect(shards)
        gain_one, query_w, key_w, value_w, out_w, gain_two, gate_w, up_w, down_w = gathered
        gain_one = gain_one.astype(jnp.float32)
        gain_two = gain_two.astype(jnp.float32)
        row_range = slice(batch_index * seq_count, (batch_index + 1) * seq_count)
        source = hidden[row_range].astype(jnp.float32)
        seg_local = segment_ids[row_range]
        inv_one = inv_rms(source)
        first_normalized = (source * inv_one * gain_one).astype(jnp.bfloat16)
        query_proj = jnp.dot(first_normalized, query_w, preferred_element_type=jnp.float32)
        projected_keys = jnp.dot(first_normalized, key_w, preferred_element_type=jnp.float32)
        projected_values = jnp.dot(first_normalized, value_w, preferred_element_type=jnp.float32)
        query_rows = rotary(
            query_proj.reshape(seq_count, span_len, local_heads, head_size), cos_heads, sin_heads
        ).astype(jnp.bfloat16)
        keys_local = rotary(projected_keys, cosine, sine_table).astype(jnp.bfloat16)
        values_local = projected_values.astype(jnp.bfloat16)
        keys_all, values_all, seg_all = (
            lax.all_gather(keys_local, "ctx", axis=1, tiled=True),
            lax.all_gather(values_local, "ctx", axis=1, tiled=True),
            lax.all_gather(seg_local.astype(jnp.bfloat16), "ctx", axis=1, tiled=True),
        )
        allowed = (seg_local[:, :, None] == seg_all.astype(jnp.int32)[:, None, :]) & causal[None]
        allowed = allowed[:, None]
        logits = (
            jnp.einsum("sqhd,skd->shqk", query_rows, keys_all, preferred_element_type=jnp.float32)
            * score_scale
        )
        logits = jnp.where(allowed, logits, NEG_FILL)
        row_peak = jnp.max(logits, axis=-1, keepdims=True)
        shifted = jnp.exp(logits - row_peak)
        totals = jnp.sum(shifted, axis=-1, keepdims=True)
        probs_low = (shifted / totals).astype(jnp.bfloat16)
        log_norm = row_peak + jnp.log(totals)
        heads_out = jnp.einsum(
            "shqk,skd->sqhd", probs_low, values_all, preferred_element_type=jnp.float32
        )
        heads_out = heads_out.reshape(seq_count, span_len, local_heads * head_size).astype(
            jnp.bfloat16
        )
        attn_out = lax.psum(jnp.dot(heads_out, out_w, preferred_element_type=jnp.float32), "tensor")
        residual = source + attn_out
        inv_two = inv_rms(residual)
        normed_two = (residual * inv_two * gain_two).astype(jnp.bfloat16)
        gate_pre = jnp.dot(normed_two, gate_w, preferred_element_type=jnp.float32)
        up_pre = jnp.dot(normed_two, up_w, preferred_element_type=jnp.float32)
        gate_sigmoid = jax.nn.sigmoid(gate_pre)
        silu_gate = gate_pre * gate_sigmoid
        activated = (silu_gate * up_pre).astype(jnp.bfloat16)
        mlp_out = lax.psum(
            jnp.dot(activated, down_w, preferred_element_type=jnp.float32).astype(jnp.bfloat16),
            "tensor",
        ).astype(jnp.float32)
        outputs.append((residual + mlp_out).astype(jnp.bfloat16))
        grad_top = cotangent[row_range]
        grad_list[8] = grad_list[8] + contract(activated, grad_top)
        d_act = project_back(grad_top, down_w)
        d_gate = (d_act * up_pre * gate_sigmoid * (1.0 + gate_pre * (1.0 - gate_sigmoid))).astype(
            jnp.bfloat16
        )
        d_up = (d_act * silu_gate).astype(jnp.bfloat16)
        grad_list[6] = grad_list[6] + contract(normed_two, d_gate)
        grad_list[7] = grad_list[7] + contract(normed_two, d_up)
        mlp_partial = project_back(d_gate, gate_w) + project_back(d_up, up_w)
        d_normed_two = lax.psum(mlp_partial, "tensor")
        d_norm_two, gain_term_two = norm_back(d_normed_two, residual, inv_two, gain_two)
        d_residual = grad_top.astype(jnp.float32) + d_norm_two
        d_residual_low = d_residual.astype(jnp.bfloat16)
        grad_list[5] = grad_list[5] + gain_term_two
        grad_list[4] = grad_list[4] + contract(heads_out, d_residual_low)
        d_heads = project_back(d_residual_low, out_w).astype(jnp.bfloat16)
        d_heads = d_heads.reshape(seq_count, span_len, local_heads, head_size)
        again = (
            jnp.einsum("sqhd,skd->shqk", query_rows, keys_all, preferred_element_type=jnp.float32)
            * score_scale
        )
        again = jnp.where(allowed, again, NEG_FILL)
        probs_again = jnp.exp(again - log_norm)
        probs_again_low = probs_again.astype(jnp.bfloat16)
        d_probs = jnp.einsum(
            "sqhd,skd->shqk", d_heads, values_all, preferred_element_type=jnp.float32
        )
        row_delta = jnp.sum(probs_again * d_probs, axis=-1, keepdims=True)
        d_scores = (probs_again * (d_probs - row_delta)).astype(jnp.bfloat16)
        d_query = (
            jnp.einsum("shqk,skd->sqhd", d_scores, keys_all, preferred_element_type=jnp.float32)
            * score_scale
        )
        key_terms = (
            jnp.einsum("shqk,sqhd->ksd", d_scores, query_rows, preferred_element_type=jnp.float32)
            * score_scale
        )
        value_terms = jnp.einsum(
            "shqk,sqhd->ksd", probs_again_low, d_heads, preferred_element_type=jnp.float32
        )
        kv_terms = jnp.stack([key_terms, value_terms], axis=1).reshape(
            seq_len, 2 * seq_count * head_size
        )
        kv_local = lax.psum_scatter(kv_terms, "ctx", scatter_dimension=0, tiled=True).reshape(
            span_len, 2, seq_count, head_size
        )
        d_key = jnp.transpose(kv_local[:, 0], (1, 0, 2))
        d_value = jnp.transpose(kv_local[:, 1], (1, 0, 2))
        d_query_proj = rotary(d_query, cos_heads, -sin_heads).astype(jnp.bfloat16)
        d_query_proj = d_query_proj.reshape(seq_count, span_len, local_heads * head_size)
        d_key_proj = rotary(d_key, cosine, -sine_table).astype(jnp.bfloat16)
        d_value_proj = d_value.astype(jnp.bfloat16)
        grad_list[1] = grad_list[1] + contract(first_normalized, d_query_proj)
        grad_list[2] = grad_list[2] + contract(first_normalized, d_key_proj)
        grad_list[3] = grad_list[3] + contract(first_normalized, d_value_proj)
        attn_partial = (
            project_back(d_query_proj, query_w)
            + project_back(d_key_proj, key_w)
            + project_back(d_value_proj, value_w)
        )
        d_normed_one = lax.psum(attn_partial, "tensor")
        d_norm_one, gain_term_one = norm_back(d_normed_one, source, inv_one, gain_one)
        grad_list[0] = grad_list[0] + gain_term_one
        input_grads.append(d_residual + d_norm_one)
    input_grad_rows = jnp.concatenate(input_grads, axis=0)
    summed = (
        lax.psum_scatter(grad_list[0], ("dp", "ctx"), scatter_dimension=0, tiled=True),
        lax.psum_scatter(grad_list[1], ("dp", "ctx"), scatter_dimension=0, tiled=True),
        lax.psum_scatter(grad_list[2], ("dp", "ctx"), scatter_dimension=0, tiled=True),
        lax.psum_scatter(grad_list[3], ("dp", "ctx"), scatter_dimension=0, tiled=True),
        lax.psum_scatter(grad_list[4], ("dp", "ctx"), scatter_dimension=1, tiled=True),
        lax.psum_scatter(grad_list[5], ("dp", "ctx"), scatter_dimension=0, tiled=True),
        lax.psum_scatter(grad_list[6], ("dp", "ctx"), scatter_dimension=0, tiled=True),
        lax.psum_scatter(grad_list[7], ("dp", "ctx"), scatter_dimension=0, tiled=True),
        lax.psum_scatter(grad_list[8], ("dp", "ctx"), scatter_dimension=1, tiled=True),
    )
    return (
        jnp.concatenate(outputs, axis=0),
        input_grad_rows,
        summed[0],
        summed[1],
        summed[2],
        summed[3],
        summed[4],
        summed[5],
        summed[6],
        summed[7],
        summed[8],
    )


def solution(mesh):
    body = per_device_general
    if tuple(mesh.shape[name] for name in AXES) == (2, 4, 4):
        body = make_fast()
    in_specs = (
        P("dp", "ctx", None),
        P("dp", "ctx", None),
        P("dp", "ctx"),
        P(("dp", "ctx")),
        P(("dp", "ctx"), "tensor"),
        P(("dp", "ctx"), "tensor"),
        P(("dp", "ctx"), "tensor"),
        P("tensor", ("dp", "ctx")),
        P(("dp", "ctx")),
        P(("dp", "ctx"), "tensor"),
        P(("dp", "ctx"), "tensor"),
        P("tensor", ("dp", "ctx")),
    )
    out_specs = (
        P("dp", "ctx", None),
        P("dp", "ctx", None),
        P(("dp", "ctx")),
        P(("dp", "ctx"), "tensor"),
        P(("dp", "ctx"), "tensor"),
        P(("dp", "ctx"), "tensor"),
        P("tensor", ("dp", "ctx")),
        P(("dp", "ctx")),
        P(("dp", "ctx"), "tensor"),
        P(("dp", "ctx"), "tensor"),
        P("tensor", ("dp", "ctx")),
    )
    return jax.shard_map(
        body, mesh=mesh, in_specs=in_specs, out_specs=out_specs, check_vma=False
    )
```
